32 devices in a mesh: head: 4 (over z), ctx: 8 (over y, x, core).
Axes of the slice: x: 2, y: 2, z: 4, core: 2. Of those that a mesh axis runs over, the one named last changes fastest.
Arguments:
- keys: bfloat16 [4096, 5120], P('ctx', 'head'), may hold values from -6 to 6
- queries: bfloat16 [4096, 5120], P('ctx', 'head'), may hold values from -6 to 6
- values: bfloat16 [4096, 5120], P('ctx', 'head'), may hold values from -6 to 6
- rates: float32 [4096, 16], P('ctx', 'head'), may hold values from 0.02 to 1
- gate_fast: float32 [16, 320, 640], P('head'), may hold values from -0.3125 to 0.3125
- up_fast: float32 [16, 320, 640], P('head'), may hold values from -0.3125 to 0.3125
- down_fast: float32 [16, 320, 640], P('head'), may hold values from -0.25 to 0.25
- out_weight: bfloat16 [5120, 5120], P('head'), may hold values from -0.078125 to 0.078125
Outputs:
- layer_out: bfloat16 [4096, 5120], P(('ctx', 'head'))
The draws below stay inside these ranges and needn't reach their ends.
All inputs are finite; a program needn't handle non-finite values.
Results may differ from the reference program's by a relative error of at most 0.011.
Values sent between devices are 32-bit elements; how exact they have to be, the bound alone decides.
A program may use at most 128 MiB of HBM per device.

```python
import math
import jax
import jax.numpy as jnp
from jax import lax

D = 5120
DH = 320
DFF = 640
NS_STEPS = 5
HEADS = 16
TOKENS = 4096


def steps_of(rng, extent, split, low, largest):
    def one(dim, blocks):
        draws = jax.random.uniform(jax.random.fold_in(jax.random.fold_in(rng, 6), dim), (blocks,), jnp.float32, low / len(split), largest / len(split))
        return jnp.repeat(jnp.exp(draws), extent[dim] // blocks).reshape((-1,) + (1,) * (len(extent) - dim - 1))

    factor_of = one(*split[0])
    for cut in split[1:]:
        factor_of = factor_of * one(*cut)
    return factor_of


def centred(rng, dims, scale, limit, split=(), kind=jnp.bfloat16):
    gain = steps_of(rng, dims, split, -0.22, 0.18) if split else 1.0
    values = jax.random.normal(rng, dims, jnp.float32) * scale * gain
    return jnp.minimum(jnp.maximum(values, -limit), limit).astype(kind)


def setup_inputs(seed: int = 0) -> dict:
    splits = jax.random.split(jax.random.key(seed), 9)
    return {
        "keys": centred(splits[0], (TOKENS, D), 1.0, 6.0, ((0, 8), (1, 4))),
        "queries": centred(splits[1], (TOKENS, D), 1.0, 6.0, ((0, 8), (1, 4))),
        "values": centred(splits[2], (TOKENS, D), 1.0, 6.0, ((0, 8), (1, 4))),
        "rates": jnp.clip(jnp.exp(math.log(1.0) - 3.912023 * jax.random.uniform(splits[3], (TOKENS, HEADS), jnp.float32) ** steps_of(splits[3], (TOKENS, HEADS), ((0, 8), (1, 4)), -0.2, 0.2)), 0.02, 1.0),
        "gate_fast": centred(splits[4], (HEADS, DH, DFF), DH ** -0.5, 0.3125, ((0, 4),), jnp.float32),
        "up_fast": centred(splits[5], (HEADS, DH, DFF), DH ** -0.5, 0.3125, ((0, 4),), jnp.float32),
        "down_fast": centred(splits[6], (HEADS, DH, DFF), DFF ** -0.5, 0.25, ((0, 4),), jnp.float32),
        "out_weight": centred(splits[7], (D, D), D ** -0.5, 0.078125, ((0, 4),)),
    }


ns_a = 3.4445
ns_b = -4.775
ns_c = 2.0315
eps_value = 1e-06

def head_grads(args):
    key_head, value_head, rate_head, gate_b, up_b, down_b = args
    gate = jnp.dot(key_head, gate_b, preferred_element_type=jnp.float32)
    upper = jnp.dot(key_head, up_b, preferred_element_type=jnp.float32)
    sig = jax.nn.sigmoid(gate)
    act = gate * sig
    hidden = (act * upper).astype(jnp.bfloat16)
    dout = (-rate_head[:, None] * value_head.astype(jnp.float32)).astype(jnp.bfloat16)
    dhid = jnp.dot(dout, down_b, preferred_element_type=jnp.float32)
    dgate = (dhid * upper * sig * (1.0 + gate * (1.0 - sig))).astype(jnp.bfloat16)
    dup = (dhid * act).astype(jnp.bfloat16)
    grad_gate = jnp.dot(key_head.T, dgate, preferred_element_type=jnp.float32)
    grad_up = jnp.dot(key_head.T, dup, preferred_element_type=jnp.float32)
    grad_down = jnp.dot(dout.T, hidden, preferred_element_type=jnp.float32)
    return jnp.stack([grad_gate, grad_up, grad_down])

def head_query(args):
    query_head, new_gate, new_up, new_down = args
    gate = jnp.dot(query_head, new_gate, preferred_element_type=jnp.float32)
    upper = jnp.dot(query_head, new_up, preferred_element_type=jnp.float32)
    hidden = (gate * jax.nn.sigmoid(gate) * upper).astype(jnp.bfloat16)
    return jnp.dot(hidden, new_down.T, preferred_element_type=jnp.float32).astype(jnp.bfloat16)

def newton(grads):
    scale = lax.rsqrt(lax.optimization_barrier(jnp.sum(grads * grads, axis=(-2, -1), keepdims=True)) + eps_value)
    iterate = grads * scale
    for sweep_index in range(NS_STEPS):
        gram = jnp.einsum('...df,...ef->...de', iterate, iterate, precision=lax.Precision.HIGHEST)
        square = jnp.einsum('...de,...ef->...df', gram, gram, precision=lax.Precision.HIGHEST)
        mixer = ns_b * gram + ns_c * square
        iterate = ns_a * iterate + jnp.einsum('...de,...ef->...df', mixer, iterate, precision=lax.Precision.HIGHEST)
    return iterate

def reference(keys, queries, values, rates, gate_fast, up_fast, down_fast, out_weight):
    key_heads = keys.reshape(TOKENS, HEADS, DH).transpose(1, 0, 2)
    value_heads = values.reshape(TOKENS, HEADS, DH).transpose(1, 0, 2)
    query_heads = queries.reshape(TOKENS, HEADS, DH).transpose(1, 0, 2)
    fast = jnp.stack([gate_fast, up_fast, down_fast])
    fast_b = fast.astype(jnp.bfloat16)
    grads = lax.map(head_grads, (key_heads, value_heads, rates.T, fast_b[0], fast_b[1], fast_b[2]))
    grads = grads.transpose(1, 0, 2, 3)
    updated = (fast - newton(grads)).astype(jnp.bfloat16)
    outputs = lax.map(head_query, (query_heads, updated[0], updated[1], updated[2]))
    joined = outputs.transpose(1, 0, 2).reshape(TOKENS, D)
    return jnp.dot(joined, out_weight, preferred_element_type=jnp.float32).astype(jnp.bfloat16)
```

```python
import functools

import jax
import jax.numpy as jnp
from jax import lax
from jax.experimental import pallas as pl
from jax.experimental.pallas import tpu as pltpu
from jax.sharding import PartitionSpec as P

NS_STEPS = 5


ns_a = 3.4445
ns_b = -4.775
ns_c = 2.0315
eps_value = 1e-06


def gram_of(iterate):
    return jnp.einsum("...df,...ef->...de", iterate, iterate, precision=lax.Precision.HIGH)


def ns_update(iterate, gram):
    square = jnp.einsum("...de,...ef->...df", gram, gram, precision=lax.Precision.HIGH)
    mixer = ns_b * gram + ns_c * square
    return ns_a * iterate + jnp.einsum(
        "...de,...ef->...df", mixer, iterate, precision=lax.Precision.HIGH
    )


def out_kernel(n, nsub, x_ref, w_hbm, o_ref, w_ref, send_buf, recv_buf, w_sem, send_sem, recv_sem):
    me = lax.axis_index("head")
    right, left = lax.rem(me + 1, n), lax.rem(me + n - 1, n)
    neighbours = (right, left)
    rows = x_ref.shape[0] // n
    half = w_ref.shape[1] // 2
    sub = half // nsub

    def columns(way, j):
        return pl.ds(way * half + j * sub, sub)

    loads = {}
    for j in range(nsub):
        for way in range(2):
            loads[way, j] = pltpu.make_async_copy(
                w_hbm.at[:, columns(way, j)], w_ref.at[:, columns(way, j)], w_sem.at[way, j]
            )
            loads[way, j].start()

    barrier = pltpu.get_barrier_semaphore()
    for neighbour in neighbours:
        pl.semaphore_signal(
            barrier, inc=1, device_id={"head": neighbour}, device_id_type=pl.DeviceIdType.MESH
        )
    pl.semaphore_wait(barrier, 2)

    def part(dest, way, j):
        block = x_ref[pl.ds(pl.multiple_of(dest * rows, rows), rows), :]
        return jnp.dot(block, w_ref[:, columns(way, j)], preferred_element_type=jnp.float32)

    copies = {}
    for s in range(n - 1):
        dests = (lax.rem(me + 2 * n - 1 - s, n), lax.rem(me + 1 + s, n))
        for j in range(nsub):
            for way in range(2):
                if s == 0:
                    loads[way, j].wait()
                total = part(dests[way], way, j)
                if s > 0:
                    copies[way, s - 1, j].wait_recv()
                    total = total + recv_buf[way, s - 1, j]
                send_buf[way, s, j] = total
                copy = pltpu.make_async_remote_copy(
                    src_ref=send_buf.at[way, s, j],
                    dst_ref=recv_buf.at[way, s, j],
                    send_sem=send_sem.at[way, s, j],
                    recv_sem=recv_sem.at[way, s, j],
                    device_id={"head": neighbours[way]},
                    device_id_type=pl.DeviceIdType.MESH,
                )
                copy.start()
                copies[way, s, j] = copy
    for j in range(nsub):
        for way in range(2):
            total = part(me, way, j)
            if n > 1:
                copies[way, n - 2, j].wait_recv()
                total = total + recv_buf[way, n - 2, j]
            o_ref[:, columns(way, j)] = total.astype(o_ref.dtype)
    for copy in copies.values():
        copy.wait_send()


def project(joined, out_weight):
    n = lax.axis_size("head")
    tokens, depth = joined.shape
    cols = out_weight.shape[1]
    nsub = 4
    rows = tokens // n
    slots = (2, n - 1, nsub, rows, cols // (2 * nsub))
    return pl.pallas_call(
        functools.partial(out_kernel, n, nsub),
        out_shape=jax.ShapeDtypeStruct((rows, cols), jnp.bfloat16),
        in_specs=[pl.BlockSpec(memory_space=pltpu.VMEM), pl.BlockSpec(memory_space=pl.ANY)],
        out_specs=pl.BlockSpec(memory_space=pltpu.VMEM),
        scratch_shapes=[
            pltpu.VMEM((depth, cols), jnp.bfloat16),
            pltpu.VMEM(slots, jnp.float32),
            pltpu.VMEM(slots, jnp.float32),
            pltpu.SemaphoreType.DMA((2, nsub)),
            pltpu.SemaphoreType.DMA((2, n - 1, nsub)),
            pltpu.SemaphoreType.DMA((2, n - 1, nsub)),
        ],
        compiler_params=pltpu.CompilerParams(collective_id=0, has_side_effects=True),
        name="project",
    )(joined, out_weight)


def body(keys, queries, values, rates, gate_fast, up_fast, down_fast, out_weight):
    rows_here = keys.shape[0]
    heads_here = gate_fast.shape[0]
    width = gate_fast.shape[1]
    hidden_width = gate_fast.shape[2]
    key_heads = keys.reshape(rows_here, heads_here, width)
    value_heads = values.reshape(rows_here, heads_here, width)
    query_heads = queries.reshape(rows_here, heads_here, width)
    fast = jnp.stack([gate_fast, up_fast, down_fast])
    fast_b = fast.astype(jnp.bfloat16)
    gate = jnp.einsum("thd,hdf->thf", key_heads, fast_b[0], preferred_element_type=jnp.float32)
    upper = jnp.einsum("thd,hdf->thf", key_heads, fast_b[1], preferred_element_type=jnp.float32)
    sig = jax.nn.sigmoid(gate)
    act = gate * sig
    hidden = (act * upper).astype(jnp.bfloat16)
    dout = (-rates[:, :, None] * value_heads.astype(jnp.float32)).astype(jnp.bfloat16)
    dhid = jnp.einsum("thd,hdf->thf", dout, fast_b[2], preferred_element_type=jnp.float32)
    dgate = (dhid * upper * sig * (1.0 + gate * (1.0 - sig))).astype(jnp.bfloat16)
    dup = (dhid * act).astype(jnp.bfloat16)
    grad_gate = jnp.einsum("thd,thf->hdf", key_heads, dgate, preferred_element_type=jnp.float32)
    grad_up = jnp.einsum("thd,thf->hdf", key_heads, dup, preferred_element_type=jnp.float32)
    grad_down = jnp.einsum("thd,thf->hdf", dout, hidden, preferred_element_type=jnp.float32)
    grads = jnp.stack([grad_gate, grad_up, grad_down])
    matrices = 3 * heads_here
    groups = lax.axis_size("ctx")
    padded_count = -(-matrices // groups) * groups
    flat = grads.reshape(matrices, width, hidden_width)
    filler = jnp.zeros((padded_count - matrices, width, hidden_width), jnp.float32)
    stacked = jnp.concatenate([flat, filler], axis=0)
    owned = lax.psum_scatter(stacked, "ctx", scatter_dimension=0, tiled=True)
    scale = lax.rsqrt(jnp.sum(owned * owned, axis=(-2, -1), keepdims=True) + eps_value)
    owned_iter = owned * scale
    for sweep_index in range(NS_STEPS):
        owned_iter = ns_update(owned_iter, gram_of(owned_iter))
    collected = lax.all_gather(owned_iter, "ctx", axis=0, tiled=True)
    iterate = collected[:matrices].reshape(3, heads_here, width, hidden_width)
    updated = (fast - iterate).astype(jnp.bfloat16)
    query_gate = jnp.einsum(
        "thd,hdf->thf", query_heads, updated[0], preferred_element_type=jnp.float32
    )
    query_up = jnp.einsum(
        "thd,hdf->thf", query_heads, updated[1], preferred_element_type=jnp.float32
    )
    query_hidden = (query_gate * jax.nn.sigmoid(query_gate) * query_up).astype(jnp.bfloat16)
    head_out = jnp.einsum(
        "thf,hdf->thd", query_hidden, updated[2], preferred_element_type=jnp.float32
    )
    joined = head_out.astype(jnp.bfloat16).reshape(rows_here, heads_here * width)
    return project(joined, out_weight)


def solution(mesh):
    in_specs = (
        P("ctx", "head"),
        P("ctx", "head"),
        P("ctx", "head"),
        P("ctx", "head"),
        P("head", None, None),
        P("head", None, None),
        P("head", None, None),
        P("head", None),
    )
    out_specs = P(("ctx", "head"), None)
    return jax.shard_map(body, mesh=mesh, in_specs=in_specs, out_specs=out_specs, check_vma=False)
```

```python
import functools

import jax
import jax.numpy as jnp
from jax import lax
from jax.experimental import pallas as pl
from jax.experimental.pallas import tpu as pltpu
from jax.sharding import PartitionSpec as P

NS_STEPS = 5


ns_a = 3.4445
ns_b = -4.775
ns_c = 2.0315
eps_value = 1e-06


def split(value):
    high = value.astype(jnp.bfloat16)
    return high, (value - high.astype(jnp.float32)).astype(jnp.bfloat16)


def product(left, right, dims):
    def one(p, q):
        return lax.dot_general(p, q, (dims, ((), ())), preferred_element_type=jnp.float32)

    return one(left[0], right[1]) + one(left[1], right[0]) + one(left[0], right[0])


def ns_step(iterate):
    parts = split(iterate)
    gram = product(parts, parts, ((1,), (1,)))
    gram_parts = split(gram)
    square = product(gram_parts, gram_parts, ((1,), (0,)))
    mixer = ns_b * gram + ns_c * square
    return ns_a * iterate + product(split(mixer), parts, ((1,), (0,)))


def flipped(chip, r):
    bit, place = 0, 1
    moved = chip
    while place <= r:
        if (r // place) % 2:
            moved = moved + (1 - 2 * ((chip // place) % 2)) * place
        place *= 2
    return moved


def newton_kernel(
    chips, per_chip, heads, g1, g3, g2, out, first, acc, rbuf, full,
    first_s, first_r, rs_s, rs_r, mid_s, mid_r, own_s, own_r, ag_s, ag_r, core_s, core_r,
):
    me = lax.axis_index("ctx")
    core, chip = me % 2, me // 2
    bits = chips.bit_length() - 1
    width = g1.shape[1]
    half, quarter = width // 2, width // 4
    per_core = -(-per_chip // 2)
    sources = (g1, g3, g2)
    matrices = 3 * heads
    partner = chip * 2 + (1 - core)
    orders = (tuple(range(bits)), tuple(reversed(range(bits))))
    sent = []

    def rows(start, size):
        return pl.ds(pl.multiple_of(start, 8), size)

    def send(src, dst, ssem, rsem, device):
        copy = pltpu.make_async_remote_copy(
            src_ref=src, dst_ref=dst, send_sem=ssem, recv_sem=rsem,
            device_id={"ctx": device}, device_id_type=pl.DeviceIdType.MESH,
        )
        copy.start()
        return copy

    def expect(ref, ssem, rsem):
        pltpu.make_async_remote_copy(
            src_ref=ref, dst_ref=ref, send_sem=ssem, recv_sem=rsem,
            device_id={"ctx": partner}, device_id_type=pl.DeviceIdType.MESH,
        ).wait_recv()

    barrier = pltpu.get_barrier_semaphore()
    peers = [partner] + [flipped(chip, 1 << b) * 2 + core for b in range(bits)]
    for peer in peers:
        pl.semaphore_signal(
            barrier, inc=1, device_id={"ctx": peer}, device_id_type=pl.DeviceIdType.MESH
        )
    pl.semaphore_wait(barrier, len(peers))

    mine, theirs = rows(core * half, half), rows((1 - core) * half, half)
    for t in range(matrices):
        sent.append(
            send(sources[t % 3].at[t // 3, theirs], first.at[t], first_s.at[t], first_r.at[t], partner)
        )
    for t in range(matrices):
        sent[t].wait_recv()
        acc[t] = sources[t % 3][t // 3, mine, :] + first[t]
    for t in range(matrices, chips * per_chip):
        acc[t] = jnp.zeros_like(acc[t])

    def live(path, s):
        return [r for r in range(chips) if all(not (r >> b) & 1 for b in orders[path][:s])]

    def ranked(path, s, taken):
        later = orders[path][s + 1 :]
        return sorted(taken, key=lambda r: [-((r >> b) & 1) for b in later])

    for s in range(bits):
        groups = []
        for path in range(2):
            b = orders[path][s]
            kept = ranked(path, s, [r for r in live(path, s) if not (r >> b) & 1])
            groups.append((path, b, kept))
        entries = [
            (path, b, kept[e], i)
            for e in range(len(groups[0][2])) for i in range(per_chip) for path, b, kept in groups
        ]
        for path, b, r, i in entries:
            goal = flipped(chip, r | (1 << b)) * per_chip + i
            part = pl.ds(path * quarter, quarter)
            sent.append(
                send(
                    acc.at[goal, part], rbuf.at[path, s, r, i], rs_s.at[path, s, r, i],
                    rs_r.at[path, s, r, i], flipped(chip, 1 << b) * 2 + core,
                )
            )
        for path, b, r, i in entries:
            slot = flipped(chip, r) * per_chip + i
            part = pl.ds(path * quarter, quarter)
            expect(rbuf.at[path, s, r, i], rs_s.at[path, s, r, i], rs_r.at[path, s, r, i])
            acc[slot, part, :] = acc[slot, part, :] + rbuf[path, s, r, i]

    for i in range(per_core):
        for which, owner in ((0, 1 - core), (1, core)):
            slot = owner * per_core + i

            @pl.when(slot < per_chip)
            def _():
                if which == 0:
                    send(
                        acc.at[chip * per_chip + slot], full.at[i, mine], mid_s.at[i], mid_r.at[i], partner
                    )
                else:
                    full[i, mine, :] = acc[chip * per_chip + slot]

    for i in range(per_core):
        slot = core * per_core + i

        @pl.when(slot < per_chip)
        def _():
            expect(full.at[i, theirs], mid_s.at[i], mid_r.at[i])
            grad = full[i]
            total = jnp.sum(jnp.sum(grad * grad, axis=0, keepdims=True), axis=1, keepdims=True)
            full[i] = grad * lax.rsqrt(total + eps_value)

            def sweep(_, carry):
                full[i] = ns_step(full[i])
                return carry

            lax.fori_loop(0, NS_STEPS, sweep, 0)
            out[chip * per_chip + slot] = full[i]
            place = out.at[chip * per_chip + slot]
            send(place, place, own_s.at[i], own_r.at[i], partner)

    for i in range(per_core):
        slot = (1 - core) * per_core + i

        @pl.when(slot < per_chip)
        def _():
            expect(out.at[chip * per_chip + slot], own_s.at[i], own_r.at[i])

    def band(path):
        return rows(core * half + path * quarter, quarter)

    for s in reversed(range(bits)):
        entries = [
            (path, orders[path][s], r, i)
            for e in range(len(live(0, s + 1))) for i in range(per_chip) for path in range(2)
            for r in [live(path, s + 1)[e]]
        ]
        for path, b, r, i in entries:
            place = out.at[flipped(chip, r) * per_chip + i, band(path)]
            there = r | (1 << b)
            sent.append(
                send(
                    place, place, ag_s.at[path, there, i], ag_r.at[path, there, i],
                    flipped(chip, 1 << b) * 2 + core,
                )
            )
        for path, b, r, i in entries:
            here = r | (1 << b)
            expect(
                out.at[flipped(chip, here) * per_chip + i, band(path)],
                ag_s.at[path, here, i], ag_r.at[path, here, i],
            )
    for r in range(1, chips):
        for i in range(per_chip):
            place = out.at[flipped(chip, r) * per_chip + i, mine]
            sent.append(send(place, place, core_s.at[r, i], core_r.at[r, i], partner))
    for r in range(1, chips):
        for i in range(per_chip):
            expect(
                out.at[flipped(chip, r) * per_chip + i, theirs], core_s.at[r, i], core_r.at[r, i]
            )
    for copy in sent:
        copy.wait_send()
    for i in range(per_core):

        @pl.when((1 - core) * per_core + i < per_chip)
        def _():
            slot = chip * per_chip + (1 - core) * per_core + i
            pltpu.make_async_remote_copy(
                src_ref=acc.at[slot], dst_ref=full.at[i, mine], send_sem=mid_s.at[i],
                recv_sem=mid_r.at[i], device_id={"ctx": partner},
                device_id_type=pl.DeviceIdType.MESH,
            ).wait_send()

        @pl.when(core * per_core + i < per_chip)
        def _():
            place = out.at[chip * per_chip + core * per_core + i]
            pltpu.make_async_remote_copy(
                src_ref=place, dst_ref=place, send_sem=own_s.at[i], recv_sem=own_r.at[i],
                device_id={"ctx": partner}, device_id_type=pl.DeviceIdType.MESH,
            ).wait_send()


def orthogonal(grad_gate, grad_up, grad_down):
    heads, width, hidden = grad_gate.shape
    chips = lax.axis_size("ctx") // 2
    per_chip = -(-3 * heads // chips)
    per_core = -(-per_chip // 2)
    bits = chips.bit_length() - 1
    slots = chips * per_chip
    dma = pltpu.SemaphoreType.DMA
    packets = (2, bits, chips, per_chip)
    vmem = pl.BlockSpec(memory_space=pltpu.VMEM)
    out = pl.pallas_call(
        functools.partial(newton_kernel, chips, per_chip, heads),
        out_shape=jax.ShapeDtypeStruct((slots, width, hidden), jnp.float32),
        in_specs=[vmem] * 3,
        out_specs=vmem,
        scratch_shapes=[
            pltpu.VMEM((3 * heads, width // 2, hidden), jnp.float32),
            pltpu.VMEM((slots, width // 2, hidden), jnp.float32),
            pltpu.VMEM(packets + (width // 4, hidden), jnp.float32),
            pltpu.VMEM((per_core, width, hidden), jnp.float32),
            dma((3 * heads,)), dma((3 * heads,)),
            dma(packets), dma(packets),
            dma((per_core,)), dma((per_core,)),
            dma((per_core,)), dma((per_core,)),
            dma((2, chips, per_chip)), dma((2, chips, per_chip)),
            dma((chips, per_chip)), dma((chips, per_chip)),
        ],
        compiler_params=pltpu.CompilerParams(collective_id=1, has_side_effects=True),
        name="orthogonal",
    )(grad_gate, grad_up, grad_down)
    return out[: 3 * heads].reshape(heads, 3, width, hidden)


def out_kernel(n, nsub, x_ref, w_hbm, o_ref, w_ref, send_buf, recv_buf, w_sem, send_sem, recv_sem):
    me = lax.axis_index("head")
    right, left = lax.rem(me + 1, n), lax.rem(me + n - 1, n)
    neighbours = (right, left)
    rows = x_ref.shape[0] // n
    half = w_ref.shape[1] // 2
    sub = half // nsub

    def columns(way, j):
        return pl.ds(way * half + j * sub, sub)

    loads = {}
    for j in range(nsub):
        for way in range(2):
            loads[way, j] = pltpu.make_async_copy(
                w_hbm.at[:, columns(way, j)], w_ref.at[:, columns(way, j)], w_sem.at[way, j]
            )
            loads[way, j].start()

    barrier = pltpu.get_barrier_semaphore()
    for neighbour in neighbours:
        pl.semaphore_signal(
            barrier, inc=1, device_id={"head": neighbour}, device_id_type=pl.DeviceIdType.MESH
        )
    pl.semaphore_wait(barrier, 2)

    def part(dest, way, j):
        block = x_ref[pl.ds(pl.multiple_of(dest * rows, rows), rows), :]
        return jnp.dot(block, w_ref[:, columns(way, j)], preferred_element_type=jnp.float32)

    copies = {}
    for s in range(n - 1):
        dests = (lax.rem(me + 2 * n - 1 - s, n), lax.rem(me + 1 + s, n))
        for j in range(nsub):
            for way in range(2):
                if s == 0:
                    loads[way, j].wait()
                total = part(dests[way], way, j)
                if s > 0:
                    copies[way, s - 1, j].wait_recv()
                    total = total + recv_buf[way, s - 1, j]
                send_buf[way, s, j] = total
                copy = pltpu.make_async_remote_copy(
                    src_ref=send_buf.at[way, s, j],
                    dst_ref=recv_buf.at[way, s, j],
                    send_sem=send_sem.at[way, s, j],
                    recv_sem=recv_sem.at[way, s, j],
                    device_id={"head": neighbours[way]},
                    device_id_type=pl.DeviceIdType.MESH,
                )
                copy.start()
                copies[way, s, j] = copy
    for j in range(nsub):
        for way in range(2):
            total = part(me, way, j)
            if n > 1:
                copies[way, n - 2, j].wait_recv()
                total = total + recv_buf[way, n - 2, j]
            o_ref[:, columns(way, j)] = total.astype(o_ref.dtype)
    for copy in copies.values():
        copy.wait_send()


def project(joined, out_weight):
    n = lax.axis_size("head")
    tokens, depth = joined.shape
    cols = out_weight.shape[1]
    nsub = 4
    rows = tokens // n
    slots = (2, n - 1, nsub, rows, cols // (2 * nsub))
    return pl.pallas_call(
        functools.partial(out_kernel, n, nsub),
        out_shape=jax.ShapeDtypeStruct((rows, cols), jnp.bfloat16),
        in_specs=[pl.BlockSpec(memory_space=pltpu.VMEM), pl.BlockSpec(memory_space=pl.ANY)],
        out_specs=pl.BlockSpec(memory_space=pltpu.VMEM),
        scratch_shapes=[
            pltpu.VMEM((depth, cols), jnp.bfloat16),
            pltpu.VMEM(slots, jnp.float32),
            pltpu.VMEM(slots, jnp.float32),
            pltpu.SemaphoreType.DMA((2, nsub)),
            pltpu.SemaphoreType.DMA((2, n - 1, nsub)),
            pltpu.SemaphoreType.DMA((2, n - 1, nsub)),
        ],
        compiler_params=pltpu.CompilerParams(collective_id=0, has_side_effects=True),
        name="project",
    )(joined, out_weight)


def body(keys, queries, values, rates, gate_fast, up_fast, down_fast, out_weight):
    rows_here = keys.shape[0]
    heads_here = gate_fast.shape[0]
    width = gate_fast.shape[1]
    hidden_width = gate_fast.shape[2]
    key_heads = keys.reshape(rows_here, heads_here, width)
    value_heads = values.reshape(rows_here, heads_here, width)
    query_heads = queries.reshape(rows_here, heads_here, width)
    fast = jnp.stack([gate_fast, up_fast, down_fast])
    fast_b = fast.astype(jnp.bfloat16)
    gate = jnp.einsum("thd,hdf->thf", key_heads, fast_b[0], preferred_element_type=jnp.float32)
    upper = jnp.einsum("thd,hdf->thf", key_heads, fast_b[1], preferred_element_type=jnp.float32)
    sig = jax.nn.sigmoid(gate)
    act = gate * sig
    hidden = (act * upper).astype(jnp.bfloat16)
    dout = (-rates[:, :, None] * value_heads.astype(jnp.float32)).astype(jnp.bfloat16)
    dhid = jnp.einsum("thd,hdf->thf", dout, fast_b[2], preferred_element_type=jnp.float32)
    dgate = (dhid * upper * sig * (1.0 + gate * (1.0 - sig))).astype(jnp.bfloat16)
    dup = (dhid * act).astype(jnp.bfloat16)
    grad_gate = jnp.einsum("thd,thf->hdf", key_heads, dgate, preferred_element_type=jnp.float32)
    grad_up = jnp.einsum("thd,thf->hdf", key_heads, dup, preferred_element_type=jnp.float32)
    grad_down = jnp.einsum("thd,thf->hdf", dout, hidden, preferred_element_type=jnp.float32)
    iterate = orthogonal(grad_gate, grad_up, grad_down)
    updated = [
        (weight - iterate[:, kind]).astype(jnp.bfloat16)
        for kind, weight in enumerate((gate_fast, up_fast, down_fast))
    ]
    query_gate = jnp.einsum(
        "thd,hdf->thf", query_heads, updated[0], preferred_element_type=jnp.float32
    )
    query_up = jnp.einsum(
        "thd,hdf->thf", query_heads, updated[1], preferred_element_type=jnp.float32
    )
    query_hidden = (query_gate * jax.nn.sigmoid(query_gate) * query_up).astype(jnp.bfloat16)
    head_out = jnp.einsum(
        "thf,hdf->thd", query_hidden, updated[2], preferred_element_type=jnp.float32
    )
    joined = head_out.astype(jnp.bfloat16).reshape(rows_here, heads_here * width)
    return project(joined, out_weight)


def solution(mesh):
    in_specs = (
        P("ctx", "head"),
        P("ctx", "head"),
        P("ctx", "head"),
        P("ctx", "head"),
        P("head", None, None),
        P("head", None, None),
        P("head", None, None),
        P("head", None),
    )
    out_specs = P(("ctx", "head"), None)
    return jax.shard_map(body, mesh=mesh, in_specs=in_specs, out_specs=out_specs, check_vma=False)
```

```python
import functools

import jax
import jax.numpy as jnp
from jax import lax
from jax.experimental import pallas as pl
from jax.experimental.pallas import tpu as pltpu
from jax.sharding import PartitionSpec as P

NS_STEPS = 5


ns_a = 3.4445
ns_b = -4.775
ns_c = 2.0315
eps_value = 1e-06


def split(value):
    high = value.astype(jnp.bfloat16)
    return high, (value - high.astype(jnp.float32)).astype(jnp.bfloat16)


def product(left, right, dims):
    def one(p, q):
        return lax.dot_general(p, q, (dims, ((), ())), preferred_element_type=jnp.float32)

    return one(left[0], right[1]) + one(left[1], right[0]) + one(left[0], right[0])


def ns_step(iterate):
    parts = split(iterate)
    gram = product(parts, parts, ((1,), (1,)))
    gram_parts = split(gram)
    square = product(gram_parts, gram_parts, ((1,), (0,)))
    mixer = ns_b * gram + ns_c * square
    return ns_a * iterate + product(split(mixer), parts, ((1,), (0,)))


def flipped(chip, r):
    bit, place = 0, 1
    moved = chip
    while place <= r:
        if (r // place) % 2:
            moved = moved + (1 - 2 * ((chip // place) % 2)) * place
        place *= 2
    return moved


def newton_kernel(
    chips, per_chip, heads, g1, g3, g2, out, first, acc, rbuf, full,
    first_s, first_r, rs_s, rs_r, mid_s, mid_r, own_s, own_r, ag_s, ag_r, core_s, core_r,
):
    me = lax.axis_index("ctx")
    core, chip = me % 2, me // 2
    bits = chips.bit_length() - 1
    width = g1.shape[1]
    half, quarter = width // 2, width // 4
    per_core = -(-per_chip // 2)
    sources = (g1, g3, g2)
    matrices = 3 * heads
    partner = chip * 2 + (1 - core)
    orders = (tuple(range(bits)), tuple(reversed(range(bits))))
    sent = []

    def rows(start, size):
        return pl.ds(pl.multiple_of(start, 8), size)

    def send(src, dst, ssem, rsem, device):
        copy = pltpu.make_async_remote_copy(
            src_ref=src, dst_ref=dst, send_sem=ssem, recv_sem=rsem,
            device_id={"ctx": device}, device_id_type=pl.DeviceIdType.MESH,
        )
        copy.start()
        return copy

    def expect(ref, ssem, rsem):
        pltpu.make_async_remote_copy(
            src_ref=ref, dst_ref=ref, send_sem=ssem, recv_sem=rsem,
            device_id={"ctx": partner}, device_id_type=pl.DeviceIdType.MESH,
        ).wait_recv()

    barrier = pltpu.get_barrier_semaphore()
    peers = [partner] + [flipped(chip, 1 << b) * 2 + core for b in range(bits)]
    for peer in peers:
        pl.semaphore_signal(
            barrier, inc=1, device_id={"ctx": peer}, device_id_type=pl.DeviceIdType.MESH
        )
    pl.semaphore_wait(barrier, len(peers))

    mine, theirs = rows(core * half, half), rows((1 - core) * half, half)
    def live(path, s):
        return [r for r in range(chips) if all(not (r >> b) & 1 for b in orders[path][:s])]

    def ranked(path, s, taken):
        later = orders[path][s:]
        return sorted(taken, key=lambda r: [-((r >> b) & 1) for b in later])

    def pass_on(path, s, r, i):
        b = orders[path][s]
        here = r - (1 << b)
        part = pl.ds(path * quarter, quarter)
        sent.append(
            send(
                acc.at[flipped(chip, r) * per_chip + i, part], rbuf.at[path, s, here, i],
                rs_s.at[path, s, here, i], rs_r.at[path, s, here, i],
                flipped(chip, 1 << b) * 2 + core,
            )
        )

    order = sorted(range(chips), key=lambda r: (-bin(r).count("1"), r))
    visits = [(r, i) for r in order for i in range(per_chip)]
    for r, i in visits:
        t = flipped(chip, r) * per_chip + i
        for kind in range(3):

            @pl.when((t < matrices) & (t % 3 == kind))
            def _():
                send(sources[kind].at[t // 3, theirs], first.at[t], first_s.at[t], first_r.at[t], partner)

    for r, i in visits:
        t = flipped(chip, r) * per_chip + i
        for kind in range(3):

            @pl.when((t < matrices) & (t % 3 == kind))
            def _():
                expect(first.at[t], first_s.at[t], first_r.at[t])
                acc[t] = sources[kind][t // 3, mine, :] + first[t]

        if matrices < chips * per_chip:

            @pl.when(t >= matrices)
            def _():
                acc[t] = jnp.zeros_like(acc[t])

        for path in range(2):
            if bits and (r >> orders[path][0]) & 1:
                pass_on(path, 0, r, i)

    for s in range(bits):
        kept = [
            ranked(path, s + 1, [r for r in live(path, s + 1)]) for path in range(2)
        ]
        for e in range(len(kept[0])):
            for i in range(per_chip):
                for path in range(2):
                    r = kept[path][e]
                    slot = flipped(chip, r) * per_chip + i
                    part = pl.ds(path * quarter, quarter)
                    expect(rbuf.at[path, s, r, i], rs_s.at[path, s, r, i], rs_r.at[path, s, r, i])
                    acc[slot, part, :] = acc[slot, part, :] + rbuf[path, s, r, i]
                    if s + 1 < bits and (r >> orders[path][s + 1]) & 1:
                        pass_on(path, s + 1, r, i)

    for i in range(per_core):
        for which, owner in ((0, 1 - core), (1, core)):
            slot = owner * per_core + i

            @pl.when(slot < per_chip)
            def _():
                if which == 0:
                    send(
                        acc.at[chip * per_chip + slot], full.at[i, mine], mid_s.at[i], mid_r.at[i], partner
                    )
                else:
                    full[i, mine, :] = acc[chip * per_chip + slot]

    def band(path):
        return rows(core * half + path * quarter, quarter)

    def link(path, s, r, slot):
        b = orders[path][s]
        place = out.at[flipped(chip, r) * per_chip + slot, band(path)]
        there = r | (1 << b)
        return pltpu.make_async_remote_copy(
            src_ref=place, dst_ref=place, send_sem=ag_s.at[path, there, slot],
            recv_sem=ag_r.at[path, there, slot],
            device_id={"ctx": flipped(chip, 1 << b) * 2 + core},
            device_id_type=pl.DeviceIdType.MESH,
        )

    def launch(slot):
        for s in reversed(range(bits)):
            for path in range(2):
                link(path, s, 0, slot).start()

    for i in range(per_core):
        slot = core * per_core + i
        other = (1 - core) * per_core + i

        @pl.when(slot < per_chip)
        def _():
            expect(full.at[i, theirs], mid_s.at[i], mid_r.at[i])
            grad = full[i]
            total = jnp.sum(jnp.sum(grad * grad, axis=0, keepdims=True), axis=1, keepdims=True)
            full[i] = grad * lax.rsqrt(total + eps_value)

            def sweep(_, carry):
                full[i] = ns_step(full[i])
                return carry

            lax.fori_loop(0, NS_STEPS, sweep, 0)
            out[chip * per_chip + slot] = full[i]
            place = out.at[chip * per_chip + slot]
            send(place, place, own_s.at[i], own_r.at[i], partner)
            launch(slot)

        @pl.when(other < per_chip)
        def _():
            expect(out.at[chip * per_chip + other], own_s.at[i], own_r.at[i])
            launch(other)

    for s in reversed(range(bits)):
        for e in range(len(live(0, s + 1))):
            for i in range(per_chip):
                for path in range(2):
                    b = orders[path][s]
                    here = live(path, s + 1)[e] | (1 << b)
                    place = out.at[flipped(chip, here) * per_chip + i, band(path)]
                    expect(place, ag_s.at[path, here, i], ag_r.at[path, here, i])
                    for later in reversed(range(s)):
                        copy = link(path, later, here, i)
                        copy.start()
                        sent.append(copy)
                    sent.append(
                        send(place, place, core_s.at[path, here, i], core_r.at[path, here, i], partner)
                    )
    for r in range(1, chips):
        for i in range(per_chip):
            for path in range(2):
                place = out.at[
                    flipped(chip, r) * per_chip + i, rows((1 - core) * half + path * quarter, quarter)
                ]
                expect(place, core_s.at[path, r, i], core_r.at[path, r, i])
    for i in range(per_chip):
        for s in range(bits):
            for path in range(2):
                link(path, s, 0, i).wait_send()
    for t in range(matrices):
        pltpu.make_async_remote_copy(
            src_ref=first.at[t], dst_ref=first.at[t], send_sem=first_s.at[t], recv_sem=first_r.at[t],
            device_id={"ctx": partner}, device_id_type=pl.DeviceIdType.MESH,
        ).wait_send()
    for copy in sent:
        copy.wait_send()
    for i in range(per_core):

        @pl.when((1 - core) * per_core + i < per_chip)
        def _():
            slot = chip * per_chip + (1 - core) * per_core + i
            pltpu.make_async_remote_copy(
                src_ref=acc.at[slot], dst_ref=full.at[i, mine], send_sem=mid_s.at[i],
                recv_sem=mid_r.at[i], device_id={"ctx": partner},
                device_id_type=pl.DeviceIdType.MESH,
            ).wait_send()

        @pl.when(core * per_core + i < per_chip)
        def _():
            place = out.at[chip * per_chip + core * per_core + i]
            pltpu.make_async_remote_copy(
                src_ref=place, dst_ref=place, send_sem=own_s.at[i], recv_sem=own_r.at[i],
                device_id={"ctx": partner}, device_id_type=pl.DeviceIdType.MESH,
            ).wait_send()


def orthogonal(grad_gate, grad_up, grad_down):
    heads, width, hidden = grad_gate.shape
    chips = lax.axis_size("ctx") // 2
    per_chip = -(-3 * heads // chips)
    per_core = -(-per_chip // 2)
    bits = chips.bit_length() - 1
    slots = chips * per_chip
    dma = pltpu.SemaphoreType.DMA
    packets = (2, bits, chips, per_chip)
    vmem = pl.BlockSpec(memory_space=pltpu.VMEM)
    out = pl.pallas_call(
        functools.partial(newton_kernel, chips, per_chip, heads),
        out_shape=jax.ShapeDtypeStruct((slots, width, hidden), jnp.float32),
        in_specs=[vmem] * 3,
        out_specs=vmem,
        scratch_shapes=[
            pltpu.VMEM((3 * heads, width // 2, hidden), jnp.float32),
            pltpu.VMEM((slots, width // 2, hidden), jnp.float32),
            pltpu.VMEM(packets + (width // 4, hidden), jnp.float32),
            pltpu.VMEM((per_core, width, hidden), jnp.float32),
            dma((3 * heads,)), dma((3 * heads,)),
            dma(packets), dma(packets),
            dma((per_core,)), dma((per_core,)),
            dma((per_core,)), dma((per_core,)),
            dma((2, chips, per_chip)), dma((2, chips, per_chip)),
            dma((2, chips, per_chip)), dma((2, chips, per_chip)),
        ],
        compiler_params=pltpu.CompilerParams(collective_id=1, has_side_effects=True),
        name="orthogonal",
    )(grad_gate, grad_up, grad_down)
    return out[: 3 * heads].reshape(heads, 3, width, hidden)


def out_kernel(n, nsub, x_ref, w_hbm, o_ref, w_ref, send_buf, recv_buf, w_sem, send_sem, recv_sem):
    me = lax.axis_index("head")
    right, left = lax.rem(me + 1, n), lax.rem(me + n - 1, n)
    neighbours = (right, left)
    rows = x_ref.shape[0] // n
    half = w_ref.shape[1] // 2
    sub = half // nsub

    def columns(way, j):
        return pl.ds(way * half + j * sub, sub)

    loads = {}
    for j in range(nsub):
        for way in range(2):
            loads[way, j] = pltpu.make_async_copy(
                w_hbm.at[:, columns(way, j)], w_ref.at[:, columns(way, j)], w_sem.at[way, j]
            )
            loads[way, j].start()

    barrier = pltpu.get_barrier_semaphore()
    for neighbour in neighbours:
        pl.semaphore_signal(
            barrier, inc=1, device_id={"head": neighbour}, device_id_type=pl.DeviceIdType.MESH
        )
    pl.semaphore_wait(barrier, 2)

    def part(dest, way, j):
        block = x_ref[pl.ds(pl.multiple_of(dest * rows, rows), rows), :]
        return jnp.dot(block, w_ref[:, columns(way, j)], preferred_element_type=jnp.float32)

    copies = {}
    for s in range(n - 1):
        dests = (lax.rem(me + 2 * n - 1 - s, n), lax.rem(me + 1 + s, n))
        for j in range(nsub):
            for way in range(2):
                if s == 0:
                    loads[way, j].wait()
                total = part(dests[way], way, j)
                if s > 0:
                    copies[way, s - 1, j].wait_recv()
                    total = total + recv_buf[way, s - 1, j]
                send_buf[way, s, j] = total
                copy = pltpu.make_async_remote_copy(
                    src_ref=send_buf.at[way, s, j],
                    dst_ref=recv_buf.at[way, s, j],
                    send_sem=send_sem.at[way, s, j],
                    recv_sem=recv_sem.at[way, s, j],
                    device_id={"head": neighbours[way]},
                    device_id_type=pl.DeviceIdType.MESH,
                )
                copy.start()
                copies[way, s, j] = copy
    for j in range(nsub):
        for way in range(2):
            total = part(me, way, j)
            if n > 1:
                copies[way, n - 2, j].wait_recv()
                total = total + recv_buf[way, n - 2, j]
            o_ref[:, columns(way, j)] = total.astype(o_ref.dtype)
    for copy in copies.values():
        copy.wait_send()


def project(joined, out_weight):
    n = lax.axis_size("head")
    tokens, depth = joined.shape
    cols = out_weight.shape[1]
    nsub = 4
    rows = tokens // n
    slots = (2, n - 1, nsub, rows, cols // (2 * nsub))
    return pl.pallas_call(
        functools.partial(out_kernel, n, nsub),
        out_shape=jax.ShapeDtypeStruct((rows, cols), jnp.bfloat16),
        in_specs=[pl.BlockSpec(memory_space=pltpu.VMEM), pl.BlockSpec(memory_space=pl.ANY)],
        out_specs=pl.BlockSpec(memory_space=pltpu.VMEM),
        scratch_shapes=[
            pltpu.VMEM((depth, cols), jnp.bfloat16),
            pltpu.VMEM(slots, jnp.float32),
            pltpu.VMEM(slots, jnp.float32),
            pltpu.SemaphoreType.DMA((2, nsub)),
            pltpu.SemaphoreType.DMA((2, n - 1, nsub)),
            pltpu.SemaphoreType.DMA((2, n - 1, nsub)),
        ],
        compiler_params=pltpu.CompilerParams(collective_id=0, has_side_effects=True),
        name="project",
    )(joined, out_weight)


def front_kernel(k_ref, v_ref, rate_ref, w1_ref, w3_ref, w2_ref, g1_ref, g3_ref, g2_ref):
    def dot(p, q, dims):
        return lax.dot_general(p, q, (dims, ((), ())), preferred_element_type=jnp.float32)

    key = k_ref[0]
    gate = dot(key, w1_ref[0].astype(jnp.bfloat16), ((1,), (0,)))
    upper = dot(key, w3_ref[0].astype(jnp.bfloat16), ((1,), (0,)))
    sig = jax.nn.sigmoid(gate)
    act = gate * sig
    hidden = (act * upper).astype(jnp.bfloat16)
    dout = (-rate_ref[0] * v_ref[0].astype(jnp.float32)).astype(jnp.bfloat16)
    dhid = dot(dout, w2_ref[0].astype(jnp.bfloat16), ((1,), (0,)))
    dgate = (dhid * upper * sig * (1.0 + gate * (1.0 - sig))).astype(jnp.bfloat16)
    dup = (dhid * act).astype(jnp.bfloat16)
    g1_ref[0] = dot(key, dgate, ((0,), (0,)))
    g3_ref[0] = dot(key, dup, ((0,), (0,)))
    g2_ref[0] = dot(dout, hidden, ((0,), (0,)))


def front(key_heads, value_heads, rates, gate_fast, up_fast, down_fast):
    heads, tokens, width = key_heads.shape
    hidden = gate_fast.shape[2]

    def block(*dims):
        return pl.BlockSpec((1,) + dims, lambda h: (h, 0, 0))

    return pl.pallas_call(
        front_kernel,
        grid=(heads,),
        out_shape=[jax.ShapeDtypeStruct((heads, width, hidden), jnp.float32)] * 3,
        in_specs=[block(tokens, width)] * 2 + [block(tokens, 1)] + [block(width, hidden)] * 3,
        out_specs=[block(width, hidden)] * 3,
        name="front",
    )(key_heads, value_heads, rates, gate_fast, up_fast, down_fast)


def body(keys, queries, values, rates, gate_fast, up_fast, down_fast, out_weight):
    rows_here = keys.shape[0]
    heads_here = gate_fast.shape[0]
    width = gate_fast.shape[1]
    key_heads = keys.reshape(rows_here, heads_here, width).transpose(1, 0, 2)
    value_heads = values.reshape(rows_here, heads_here, width).transpose(1, 0, 2)
    query_heads = queries.reshape(rows_here, heads_here, width)
    grad_gate, grad_up, grad_down = front(
        key_heads, value_heads, rates.T[:, :, None], gate_fast, up_fast, down_fast
    )
    iterate = orthogonal(grad_gate, grad_up, grad_down)
    updated = [
        (weight - iterate[:, kind]).astype(jnp.bfloat16)
        for kind, weight in enumerate((gate_fast, up_fast, down_fast))
    ]
    query_gate = jnp.einsum(
        "thd,hdf->thf", query_heads, updated[0], preferred_element_type=jnp.float32
    )
    query_up = jnp.einsum(
        "thd,hdf->thf", query_heads, updated[1], preferred_element_type=jnp.float32
    )
    query_hidden = (query_gate * jax.nn.sigmoid(query_gate) * query_up).astype(jnp.bfloat16)
    head_out = jnp.einsum(
        "thf,hdf->thd", query_hidden, updated[2], preferred_element_type=jnp.float32
    )
    joined = head_out.astype(jnp.bfloat16).reshape(rows_here, heads_here * width)
    return project(joined, out_weight)


def solution(mesh):
    in_specs = (
        P("ctx", "head"),
        P("ctx", "head"),
        P("ctx", "head"),
        P("ctx", "head"),
        P("head", None, None),
        P("head", None, None),
        P("head", None, None),
        P("head", None),
    )
    out_specs = P(("ctx", "head"), None)
    return jax.shard_map(body, mesh=mesh, in_specs=in_specs, out_specs=out_specs, check_vma=False)
```
